32 devices in a mesh: groups: 2 (over y), dp: 4 (over x, core), member: 4 (over z).
Axes of the slice: x: 2, y: 2, z: 4, core: 2. Of those that a mesh axis runs over, the one named last changes fastest.
Arguments:
- context: bfloat16 [4096, 1024], P(('groups', 'dp', 'member')), parts along dimension 0, may hold values from -6 to 6
- residual: bfloat16 [4096, 1024], P(('groups', 'dp', 'member')), parts along dimension 0, may hold values from -6 to 6
- proj_weight: bfloat16 [1024, 1024], P('member'), may hold values from -0.1875 to 0.1875
- head_weights: bfloat16 [4, 1024, 1024], P('member'), may hold values from -0.1875 to 0.1875
- boot: int32 [128, 4], P(('groups', 'dp', 'member')), parts along dimension 0, may hold values from 0 to 4, as said below
Outputs:
- grad_context: bfloat16 [4096, 1024], P(('groups', 'dp', 'member')), parts along dimension 0
- grad_residual: bfloat16 [4096, 1024], P(('groups', 'dp', 'member')), parts along dimension 0
- grad_proj: float32 [2048, 1024], P(('groups', 'member')), parts along dimension 0
- grad_heads: float32 [8, 1024, 1024], P(('groups', 'member'), 'dp'), parts along dimension 0
The draws below stay inside these ranges and needn't reach their ends.
There are 2 independent parts, one for each index of `groups`. The reference program is written for one: setup_inputs(seed, part) draws one part's arguments, and reference() takes and returns one part's arrays. A program takes and returns all parts, laid end to end along the dimension named above; an argument that names none is the same for every part. Nothing has to cross between parts.
Inputs may be any that keep to these rules, and one draw needn't show every extreme that they name: `boot`: among the 4 blocks of one device at most 2 have a nonzero weight for any one head. Every device has exactly 2 such blocks for some head, and in every draw some head gets exactly 2 from every device of one index of dp. Weights follow a Poisson law of mean one, cut at 4.
All inputs are finite; a program needn't handle non-finite values.
Results may differ from the reference program's by a relative error of at most 0.013.
Values may be sent and summed in bfloat16 or wider, within the bound.
A program may use at most 64 MiB of HBM per device.

```python
import jax
import jax.numpy as jnp
from jax import lax

D = 1024
POOL = 2
BLOCK = 16
BLK_DEV = 4
CAP = 2
HEADS = 4
BLOCKS = 64
TOKENS = 2048
N_DP = 4
N_MEMBER = 4


def draw_boot(key, part):
    raw_bits = jax.random.randint(jax.random.fold_in(key, 11), (BLOCKS, HEADS), 0, 1048576)
    poisson_draw = (raw_bits >= 385749).astype(jnp.int32) + (raw_bits >= 771499).astype(jnp.int32)
    poisson_draw = poisson_draw + (raw_bits >= 964358).astype(jnp.int32) + (raw_bits >= 1028605).astype(jnp.int32)
    block_owner = jnp.arange(BLOCKS, dtype=jnp.int32) // BLK_DEV
    head_ids = jnp.arange(HEADS, dtype=jnp.int32)
    shift_head = jax.random.randint(jax.random.fold_in(key, 12), (), 0, HEADS)
    full_head = jax.random.randint(jax.random.fold_in(key, 13), (), 0, HEADS)
    full_row = jax.random.randint(jax.random.fold_in(key, 14), (), 0, BLOCKS // (BLK_DEV * HEADS))
    forced_one = (block_owner[:, None] + shift_head) % HEADS == head_ids[None, :]
    forced_two = (block_owner[:, None] // HEADS == full_row) & (head_ids[None, :] == full_head)
    poisson_draw = jnp.where(forced_one | forced_two, jnp.maximum(poisson_draw, 1), poisson_draw)
    live_mask = (poisson_draw > 0).astype(jnp.int32).reshape(BLOCKS // BLK_DEV, BLK_DEV, HEADS)
    live_rank = jnp.cumsum(live_mask, axis=1).reshape(BLOCKS, HEADS)
    return jnp.where(live_rank <= CAP, poisson_draw, 0).astype(jnp.int32)


def level_of(rng, extent, shards, least, largest):
    loudness = 1.0
    for position, shards_of in shards:
        heights = jax.random.uniform(jax.random.fold_in(jax.random.fold_in(rng, 6), position), (shards_of,), jnp.float32, least / len(shards), largest / len(shards))
        loudness = loudness * jnp.repeat(jnp.exp(heights), extent[position] // shards_of).reshape((-1,) + (1,) * (len(extent) - 1 - position))
    return loudness


def noise(own_key, extent, deviation, bound, shards=(), kind=jnp.bfloat16):
    factor_of = level_of(own_key, extent, shards, -0.22, 0.18) if shards else 1.0
    drawn = jax.random.normal(own_key, extent, jnp.float32) * deviation * factor_of
    return jnp.minimum(jnp.maximum(drawn, -bound), bound).astype(kind)


def setup_inputs(seed: int = 0, part: int = 0) -> dict:
    arg_keys = jax.random.split(jax.random.key(seed), 6)
    part_splits = jax.random.split(jax.random.fold_in(arg_keys[5], part), 6)
    return {
        "context": noise(part_splits[0], (TOKENS, D), 1.0, 6.0, ((0, 16),)),
        "residual": noise(part_splits[1], (TOKENS, D), 1.0, 6.0, ((0, 16),)),
        "proj_weight": noise(arg_keys[2], (D, D), D ** -0.5, 0.1875, ((0, 4),)),
        "head_weights": noise(arg_keys[3], (HEADS, D, D), D ** -0.5, 0.1875, ((0, 4),)),
        "boot": draw_boot(jax.random.fold_in(jax.random.fold_in(arg_keys[5], part), 71), part),
    }


EPS = 1e-06

def gelu_tanh(pre_value):
    return jax.nn.gelu(pre_value, approximate=True)

def slot_table(weights):
    live_mask = (weights > 0).astype(jnp.int32)
    live_rank = jnp.cumsum(live_mask, axis=-1) - 1
    slot_ids = jnp.arange(CAP, dtype=jnp.int32)
    picked = live_mask[..., None, :] * (live_rank[..., None, :] == slot_ids[:, None]).astype(jnp.int32)
    slot_weight = lax.optimization_barrier(jnp.sum(picked * weights[..., None, :], axis=-1))
    return (picked, slot_weight)

def head_pass(block_rows, slot_weight, weight, head_count):
    block_rows = block_rows.astype(jnp.float32)
    model_width = block_rows.shape[-1]
    flat_rows = block_rows.reshape(-1, model_width)
    inverse = lax.rsqrt(lax.optimization_barrier(jnp.mean(flat_rows * flat_rows, axis=-1, keepdims=True)) + EPS)
    normed = flat_rows * inverse
    normed_low = normed.astype(jnp.bfloat16)
    pre_act = jnp.dot(normed_low, weight, preferred_element_type=jnp.float32)
    activated, back_act = jax.vjp(gelu_tanh, pre_act)
    pred = (flat_rows + activated).reshape(block_rows.shape)
    error_rows = pred[:, :, :-1] - block_rows[:, :, 1:]
    error_rows = jnp.concatenate([error_rows, jnp.zeros_like(error_rows[:, :, :1])], axis=2)
    row_scale = slot_weight.astype(jnp.float32) / head_count
    d_pred = (error_rows * row_scale[:, :, None, None]).reshape(flat_rows.shape)
    d_pre_low = back_act(d_pred)[0].astype(jnp.bfloat16)
    d_normed = lax.dot_general(d_pre_low, weight, (((1,), (1,)), ((), ())), preferred_element_type=jnp.float32)
    d_rows = d_pred + inverse * (d_normed - normed * lax.optimization_barrier(jnp.mean(d_normed * normed, axis=-1, keepdims=True)))
    return (normed_low, d_pre_low, d_rows.astype(jnp.bfloat16).reshape(block_rows.shape))

def reference(context, residual, proj_weight, head_weights, boot):
    devices = N_DP * N_MEMBER
    hidden = residual.astype(jnp.float32) + jnp.dot(context, proj_weight, preferred_element_type=jnp.float32)
    latent = lax.optimization_barrier(jnp.mean(hidden.reshape(-1, POOL, D), axis=1)).astype(jnp.bfloat16)
    latent_wide = latent.reshape(devices, BLK_DEV, BLOCK, D).astype(jnp.float32)

    def per_head(grad_carry, inputs):
        weight, column = inputs
        picked, slot_weight = slot_table(column.reshape(devices, BLK_DEV))
        picked_wide = picked.astype(jnp.float32)
        block_rows = jnp.einsum('gsk,gkrd->gsrd', picked_wide, latent_wide)
        normed_low, d_pre_low, d_rows = head_pass(block_rows, slot_weight, weight, HEADS)
        left_side = normed_low.reshape(N_DP, -1, D).astype(jnp.float32)
        right_side = d_pre_low.reshape(N_DP, -1, D).astype(jnp.float32)
        partial_sums = jnp.einsum('nrk,nrj->nkj', left_side, right_side)
        partial_sums = lax.optimization_barrier(partial_sums.astype(jnp.bfloat16)).astype(jnp.float32)
        grad_head = lax.optimization_barrier(jnp.sum(partial_sums, axis=0))
        grad_carry = grad_carry + jnp.einsum('gsk,gsrd->gkrd', picked_wide, d_rows.astype(jnp.float32))
        return (grad_carry, grad_head)
    start_grad = jnp.zeros((devices, BLK_DEV, BLOCK, D), jnp.float32)
    grad_latent, grad_heads = lax.scan(per_head, start_grad, (head_weights, boot.T))
    grad_tokens = jnp.repeat(grad_latent.reshape(-1, D), POOL, axis=0) / POOL
    grad_low = grad_tokens.astype(jnp.bfloat16)
    grad_context = lax.dot_general(grad_low, proj_weight, (((1,), (1,)), ((), ())), preferred_element_type=jnp.float32).astype(jnp.bfloat16)

    def per_device(running, pieces):
        context_piece, grad_piece = pieces
        partial_term = lax.dot_general(context_piece, grad_piece, (((0,), (0,)), ((), ())), preferred_element_type=jnp.float32)
        return (running + lax.optimization_barrier(partial_term.astype(jnp.bfloat16)).astype(jnp.float32), None)
    grad_proj, _ = lax.scan(per_device, jnp.zeros((D, D), jnp.float32), (context.reshape(devices, -1, D), grad_low.reshape(devices, -1, D)))
    return (grad_context, grad_low, grad_proj, grad_heads)
```

```python
import functools

import jax
import jax.numpy as jnp
from jax import lax
from jax.experimental import pallas as pl
from jax.experimental.pallas import tpu as pltpu
from jax.sharding import PartitionSpec as P

POOL = 2
BLOCK = 16
BLK_DEV = 4
CAP = 2


EPS = 1e-06


def gelu_tanh(pre_value):
    return jax.nn.gelu(pre_value, approximate=True)


def slot_table(weights):
    live_mask = (weights > 0).astype(jnp.int32)
    live_rank = jnp.cumsum(live_mask, axis=-1) - 1
    slot_ids = jnp.arange(CAP, dtype=jnp.int32)
    picked = live_mask[..., None, :] * (live_rank[..., None, :] == slot_ids[:, None]).astype(
        jnp.int32
    )
    slot_weight = jnp.sum(picked * weights[..., None, :], axis=-1)
    return (picked, slot_weight)


def head_pass(block_rows, slot_weight, weight, head_count):
    block_rows = block_rows.astype(jnp.float32)
    model_width = block_rows.shape[-1]
    flat_rows = block_rows.reshape(-1, model_width)
    inverse = lax.rsqrt(jnp.mean(flat_rows * flat_rows, axis=-1, keepdims=True) + EPS)
    normed = flat_rows * inverse
    normed_low = normed.astype(jnp.bfloat16)
    pre_act = jnp.dot(normed_low, weight, preferred_element_type=jnp.float32)
    activated, back_act = jax.vjp(gelu_tanh, pre_act)
    pred = (flat_rows + activated).reshape(block_rows.shape)
    error_rows = pred[:, :, :-1] - block_rows[:, :, 1:]
    error_rows = jnp.concatenate([error_rows, jnp.zeros_like(error_rows[:, :, :1])], axis=2)
    row_scale = slot_weight.astype(jnp.float32) / head_count
    d_pred = (error_rows * row_scale[:, :, None, None]).reshape(flat_rows.shape)
    d_pre_low = back_act(d_pred)[0].astype(jnp.bfloat16)
    d_normed = lax.dot_general(
        d_pre_low, weight, (((1,), (1,)), ((), ())), preferred_element_type=jnp.float32
    )
    d_rows = d_pred + inverse * (
        d_normed - normed * jnp.mean(d_normed * normed, axis=-1, keepdims=True)
    )
    return (normed_low, d_pre_low, d_rows.astype(jnp.bfloat16).reshape(block_rows.shape))


def local(context, residual, proj_weight, head_weights, boot):
    members = lax.axis_size("member")
    fits = lax.axis_size("dp") == 4 and lax.axis_size("groups") == 2
    if fits and boot.shape[1] == members and context.shape[1] % (256 * members) == 0:
        return fused(context, residual, proj_weight, head_weights, boot)
    head_count = boot.shape[1]
    model_width = context.shape[1]
    own_index = lax.axis_index("member")
    whole_proj = lax.all_gather(proj_weight, "member", axis=0, tiled=True)
    hidden = residual.astype(jnp.float32) + jnp.dot(
        context, whole_proj, preferred_element_type=jnp.float32
    )
    latent = jnp.mean(hidden.reshape(BLK_DEV * BLOCK, POOL, model_width), axis=1).astype(
        jnp.bfloat16
    )
    latent = latent.reshape(BLK_DEV, BLOCK, model_width)
    picked_out, weight_out = slot_table(boot.T)
    all_latent, all_boot = (
        lax.all_gather(latent, "member", axis=0, tiled=True),
        lax.all_gather(boot, "member", axis=0, tiled=True),
    )
    own_mask = (jnp.arange(head_count, dtype=jnp.int32) == own_index).astype(jnp.int32)
    column = jnp.sum(all_boot * own_mask[None, :], axis=1).reshape(members, BLK_DEV)
    picked_in, weight_in = slot_table(column)
    all_latent = all_latent.reshape(members, BLK_DEV, BLOCK, model_width)
    received = jnp.einsum(
        "jsk,jkrd->jsrd",
        picked_in.astype(jnp.bfloat16),
        all_latent,
        preferred_element_type=jnp.float32,
    ).astype(jnp.bfloat16)
    weight = head_weights[0]
    normed_low, d_pre_low, d_rows = head_pass(received, weight_in, weight, head_count)
    columns = normed_low
    grad_head = lax.psum_scatter(
        lax.dot_general(
            columns, d_pre_low, (((0,), (0,)), ((), ())), preferred_element_type=jnp.float32
        ).astype(jnp.bfloat16),
        "dp",
        scatter_dimension=0,
        tiled=True,
    ).astype(jnp.float32)
    returned = lax.all_to_all(d_rows, "member", split_axis=0, concat_axis=0, tiled=True)
    grad_latent = jnp.einsum(
        "hsk,hsrd->krd",
        picked_out.astype(jnp.bfloat16),
        returned,
        preferred_element_type=jnp.float32,
    )
    grad_tokens = jnp.broadcast_to(
        grad_latent.reshape(BLK_DEV * BLOCK, 1, model_width) / POOL,
        (BLK_DEV * BLOCK, POOL, model_width),
    )
    grad_low = grad_tokens.reshape(-1, model_width).astype(jnp.bfloat16)
    grad_context = lax.dot_general(
        grad_low, whole_proj, (((1,), (1,)), ((), ())), preferred_element_type=jnp.float32
    )
    columns = context
    grad_proj = lax.psum_scatter(
        lax.dot_general(
            columns, grad_low, (((0,), (0,)), ((), ())), preferred_element_type=jnp.float32
        ).astype(jnp.bfloat16),
        "member",
        scatter_dimension=0,
        tiled=True,
    ).astype(jnp.float32)
    grad_proj = lax.psum(grad_proj.astype(jnp.bfloat16), "dp").astype(jnp.float32)
    return (grad_context.astype(jnp.bfloat16), grad_low, grad_proj, grad_head[None])


MESH = pl.DeviceIdType.MESH
F32 = jnp.float32
BF16 = jnp.bfloat16
LANES = 128
ROW_DEV = BLK_DEV * BLOCK
ROW_SLOT = CAP * BLOCK


def picks(boot_ref, head):
    weights = [boot_ref[k, head] for k in range(BLK_DEV)]
    live = [jnp.where(w > 0, 1, 0) for w in weights]
    factor = [[None] * BLK_DEV for _ in range(CAP)]
    slot = [0] * CAP
    rank = 0
    for k in range(BLK_DEV):
        for s in range(CAP):
            hit = live[k] * jnp.where(rank == s, 1, 0)
            factor[s][k] = hit.astype(F32)
            slot[s] = slot[s] + hit * weights[k]
        rank = rank + live[k]
    return factor, [w.astype(F32) for w in slot]


def step_kernel(
    n,
    context_ref, residual_ref, proj_ref, head_ref, boot_ref,
    gctx_ref, gres_ref, gproj_ref, ghead_ref,
    whole, pool, poolg, msg, xin, nbuf, ng, dg, dxs, dxin, gg, pout, pin, tout, tin,
    z_send, z_recv, pc_send, pc_recv, pl_send, pl_recv, co_send, co_recv,
    ms_send, ms_recv, n_send, n_recv, d_send, d_recv, dx_send, dx_recv,
    g_send, g_recv, r_send, r_recv,
):
    group, dp, me = lax.axis_index("groups"), lax.axis_index("dp"), lax.axis_index("member")
    width = context_ref.shape[1]
    part = width // n
    cut = part // 8
    core = lax.rem(dp, 2)
    mate = dp + 1 - 2 * core
    across = lax.rem(dp + 2, 4)
    across_mate = lax.rem(mate + 2, 4)
    other = 1 - group

    def copy(src, dst, send, recv, g=None, d=None, m=None):
        return pltpu.make_async_remote_copy(
            src_ref=src, dst_ref=dst, send_sem=send, recv_sem=recv,
            device_id=(group if g is None else g, dp if d is None else d, me if m is None else m),
            device_id_type=MESH,
        )

    def piece(owner, g, d):
        return pl.ds(pl.multiple_of(owner * part + (g * 4 + d) * cut, cut), cut)

    def cols(index):
        return pl.ds(pl.multiple_of(index * part, part), part)

    barrier = pltpu.get_barrier_semaphore()
    peers = [(group, dp, lax.rem(me + r, n)) for r in range(1, n)]
    peers += [(group, d, me) for d in (mate, across, across_mate)]
    peers += [(other, d, me) for d in (dp, across)]
    for peer in peers:
        pl.semaphore_signal(barrier, inc=1, device_id=peer, device_id_type=MESH)

    tokens = context_ref.shape[0]
    first = lax.broadcasted_iota(jnp.int32, (ROW_DEV, tokens), 0) * 2
    gap = lax.broadcasted_iota(jnp.int32, (ROW_DEV, tokens), 1) - first
    pair = jnp.where((gap >= 0) & (gap < 2), 1.0, 0.0).astype(BF16)
    pool[...] = jnp.dot(pair, context_ref[...], preferred_element_type=F32).astype(BF16)
    pl.semaphore_wait(barrier, len(peers))

    own_piece = pl.ds(pl.multiple_of((group * 4 + dp) * cut, cut), cut)
    pending = []
    for r in range(1, n):
        z = copy(proj_ref.at[own_piece], whole.at[piece(me, group, dp)], z_send.at[r - 1], z_recv.at[r - 1],
                 m=lax.rem(me + r, n))
        z.start()
        pending.append(z)
    pool_copies = []
    for r in range(1, n):
        c = copy(pool.at[:, cols(lax.rem(me + r, n))], poolg.at[me], pc_send.at[r - 1], pc_recv.at[r - 1],
                 m=lax.rem(me + r, n))
        c.start()
        pool_copies.append(c)
    poolg[me] = pool[:, cols(me)]
    whole[cols(me), :] = proj_ref[...]
    total = jnp.dot(pair, residual_ref[...], preferred_element_type=F32)
    total += jnp.dot(pool[:, cols(me)], proj_ref[...], preferred_element_type=F32)

    spots = [(group, across), (other, dp), (other, across)]
    order = [1, n - 1] + list(range(2, n - 1))
    plane, sides = {}, {}
    for r in order:
        owner = lax.rem(me + n - r, n)
        pending[r - 1].wait_recv()
        here = whole.at[piece(owner, group, dp)]
        for t, (g, d) in enumerate(spots):
            plane[r, t] = copy(here, here, pl_send.at[r - 1, t], pl_recv.at[r - 1, t], g=g, d=d)
            plane[r, t].start()
        sides[r, 3] = copy(here, here, co_send.at[r - 1, 3], co_recv.at[r - 1, 3], d=mate)
        sides[r, 3].start()
    for r in order:
        owner = lax.rem(me + n - r, n)
        for t, (g, d) in enumerate(spots):
            plane[r, t].wait_recv()
            there = whole.at[piece(owner, g, d)]
            sides[r, t] = copy(there, there, co_send.at[r - 1, t], co_recv.at[r - 1, t], d=mate)
            sides[r, t].start()
    for r in order:
        owner = lax.rem(me + n - r, n)
        for t in range(4):
            sides[r, t].wait_recv()
        total += jnp.dot(pool[:, cols(owner)], whole[cols(owner), :], preferred_element_type=F32)
    latent = (total * 0.5).astype(BF16).astype(F32)

    factors = []
    sends = []
    for r in list(range(1, n)) + [0]:
        head = lax.rem(me + r, n)
        factor, slot = picks(boot_ref, head)
        factors.append((head, factor))
        for s in range(CAP):
            rows = slice(s * BLOCK, (s + 1) * BLOCK)
            block = factor[s][0] * latent[:BLOCK]
            for k in range(1, BLK_DEV):
                block += factor[s][k] * latent[k * BLOCK : (k + 1) * BLOCK]
            scale = jnp.zeros((BLOCK, LANES), F32) + slot[s]
            if r:
                msg[r - 1, rows, :width] = block.astype(BF16)
                msg[r - 1, rows, width:] = scale.astype(BF16)
            else:
                xin[me, rows, :width] = block.astype(BF16)
                xin[me, rows, width:] = scale.astype(BF16)
        if r:
            c = copy(msg.at[r - 1], xin.at[me], ms_send.at[r - 1], ms_recv.at[r - 1], m=head)
            c.start()
            sends.append(c)
    for c in sends:
        c.wait_recv()

    count = n * ROW_SLOT
    x = xin[:, :, :width].reshape(count, width).astype(F32)
    scale = xin[:, :, width:].reshape(count, LANES).astype(F32)[:, :1] / n
    inverse = lax.rsqrt(jnp.mean(x * x, axis=-1, keepdims=True) + EPS)
    normed = x * inverse
    nbuf[0] = normed.astype(BF16)
    ng[dp] = nbuf[0, :, pl.ds(pl.multiple_of(dp * (width // 4), width // 4), width // 4)]
    n_copies = []
    for t, d in enumerate((across, across_mate, mate)):
        c = copy(nbuf.at[0, :, pl.ds(pl.multiple_of(d * (width // 4), width // 4), width // 4)], ng.at[dp],
                 n_send.at[t], n_recv.at[t], d=d)
        c.start()
        n_copies.append(c)
    pre = jnp.dot(nbuf[0], head_ref[0], preferred_element_type=F32)
    root, cubic = 0.7978845608028654, 0.044715
    bent = jnp.tanh(root * (pre + cubic * pre * pre * pre))
    active = 0.5 * pre * (1.0 + bent)
    slope = 0.5 * (1.0 + bent) + 0.5 * pre * (1.0 - bent * bent) * (root * (1.0 + 3.0 * cubic * pre * pre))
    place = lax.broadcasted_iota(jnp.int32, (count, 1), 0)
    keep = jnp.where((place & (BLOCK - 1)) == BLOCK - 1, 0.0, 1.0)
    after = pltpu.roll(x, count - 1, 0)
    d_pred = (x + active - after) * (scale * keep)
    dg[dp] = (d_pred * slope).astype(BF16)
    d_copies = []
    for t, d in enumerate((across, mate)):
        c = copy(dg.at[dp], dg.at[dp], d_send.at[t], d_recv.at[t], d=d)
        c.start()
        d_copies.append(c)
    d_normed = lax.dot_general(dg[dp], head_ref[0], (((1,), (1,)), ((), ())), preferred_element_type=F32)
    d_rows = d_pred + inverse * (d_normed - normed * jnp.mean(d_normed * normed, axis=-1, keepdims=True))
    dxs[...] = d_rows.astype(BF16).reshape(n, ROW_SLOT, width)
    dxin[me] = dxs[me]
    dx_copies = []
    for r in range(1, n):
        peer = lax.rem(me + r, n)
        c = copy(dxs.at[peer], dxin.at[me], dx_send.at[r - 1], dx_recv.at[r - 1], m=peer)
        c.start()
        dx_copies.append(c)
    d_copies[0].wait_recv()
    forward = copy(dg.at[across], dg.at[across], d_send.at[2], d_recv.at[2], d=mate)
    forward.start()
    for c in dx_copies:
        c.wait_recv()

    rows = [jnp.zeros((BLOCK, width), F32) for _ in range(BLK_DEV)]
    for head, factor in factors:
        back = dxin[head].astype(F32)
        for k in range(BLK_DEV):
            for s in range(CAP):
                rows[k] += factor[s][k] * back[s * BLOCK : (s + 1) * BLOCK]
    for k in range(BLK_DEV):
        gg[me, k * BLOCK : (k + 1) * BLOCK, :] = (rows[k] * (1.0 / POOL)).astype(BF16)
    g_copies = []
    for r in range(1, n):
        c = copy(gg.at[me], gg.at[me], g_send.at[r - 1], g_recv.at[r - 1], m=lax.rem(me + r, n))
        c.start()
        g_copies.append(c)

    repeat = lax.broadcasted_iota(jnp.int32, (tokens, ROW_DEV), 1) * 2
    gap = lax.broadcasted_iota(jnp.int32, (tokens, ROW_DEV), 0) - repeat
    spread = jnp.where((gap >= 0) & (gap < 2), 1.0, 0.0).astype(BF16)
    grad = gg[me]
    gres_ref[...] = jnp.dot(spread, grad, preferred_element_type=F32).astype(BF16)
    gctx = lax.dot_general(grad, whole[...], (((1,), (1,)), ((), ())), preferred_element_type=F32)
    gctx_ref[...] = jnp.dot(spread, gctx.astype(BF16), preferred_element_type=F32).astype(BF16)
    for c in n_copies:
        c.wait_recv()
    d_copies[1].wait_recv()
    forward.wait_recv()
    ghead_ref[0] = lax.dot_general(
        ng[...].reshape(4 * count, width // 4), dg[...].reshape(4 * count, width),
        (((0,), (0,)), ((), ())), preferred_element_type=F32)

    for c in pool_copies:
        c.wait_recv()
    for c in g_copies:
        c.wait_recv()
    half = part // 2
    mine = pl.ds(pl.multiple_of(core * half, half), half)
    theirs = pl.ds(pl.multiple_of((1 - core) * half, half), half)
    gproj_ref[...] = lax.dot_general(
        poolg[...].reshape(n * ROW_DEV, part), gg[...].reshape(n * ROW_DEV, width),
        (((0,), (0,)), ((), ())), preferred_element_type=F32)
    pout[...] = gproj_ref[theirs, :].astype(BF16)
    a = copy(pout, pin, r_send.at[0], r_recv.at[0], d=mate)
    a.start()
    a.wait_recv()
    tout[...] = (gproj_ref[mine, :] + pin[...].astype(F32)).astype(BF16)
    b = copy(tout, tin, r_send.at[1], r_recv.at[1], d=across)
    b.start()
    b.wait_recv()
    gproj_ref[mine, :] = tout[...].astype(F32) + tin[...].astype(F32)
    c = copy(gproj_ref.at[mine], gproj_ref.at[mine], r_send.at[2], r_recv.at[2], d=mate)
    c.start()
    c.wait_recv()
    for copies in (pending, pool_copies, plane.values(), sides.values(), sends, n_copies, d_copies, dx_copies, g_copies):
        for c2 in copies:
            c2.wait_send()
    for c2 in (forward, a, b, c):
        c2.wait_send()


def fused(context, residual, proj_weight, head_weights, boot):
    n = lax.axis_size("member")
    tokens, width = context.shape
    count = n * ROW_SLOT
    part = width // n
    vmem = pl.BlockSpec(memory_space=pltpu.VMEM)
    dma = pltpu.SemaphoreType.DMA
    peer = dma((n - 1,))
    return pl.pallas_call(
        functools.partial(step_kernel, n),
        out_shape=(
            jax.ShapeDtypeStruct((tokens, width), BF16),
            jax.ShapeDtypeStruct((tokens, width), BF16),
            jax.ShapeDtypeStruct((part, width), F32),
            jax.ShapeDtypeStruct((1, width // 4, width), F32),
        ),
        in_specs=[vmem] * 4 + [pl.BlockSpec(memory_space=pltpu.SMEM)],
        out_specs=(vmem,) * 4,
        scratch_shapes=[
            pltpu.VMEM((width, width), BF16),
            pltpu.VMEM((ROW_DEV, width), BF16),
            pltpu.VMEM((n, ROW_DEV, part), BF16),
            pltpu.VMEM((n - 1, ROW_SLOT, width + LANES), BF16),
            pltpu.VMEM((n, ROW_SLOT, width + LANES), BF16),
            pltpu.VMEM((1, count, width), BF16),
            pltpu.VMEM((4, count, width // 4), BF16),
            pltpu.VMEM((4, count, width), BF16),
            pltpu.VMEM((n, ROW_SLOT, width), BF16),
            pltpu.VMEM((n, ROW_SLOT, width), BF16),
            pltpu.VMEM((n, ROW_DEV, width), BF16),
            pltpu.VMEM((part // 2, width), BF16),
            pltpu.VMEM((part // 2, width), BF16),
            pltpu.VMEM((part // 2, width), BF16),
            pltpu.VMEM((part // 2, width), BF16),
            peer, peer, peer, peer,
            dma((n - 1, 3)), dma((n - 1, 3)), dma((n - 1, 4)), dma((n - 1, 4)),
            peer, peer, dma((3,)), dma((3,)), dma((3,)), dma((3,)), peer, peer,
            peer, peer, dma((3,)), dma((3,)),
        ],
        compiler_params=pltpu.CompilerParams(
            collective_id=0, has_side_effects=True, vmem_limit_bytes=56 * 2**20
        ),
        name="step",
    )(context, residual, proj_weight, head_weights, boot)


def solution(mesh):
    in_specs = (
        P(("groups", "dp", "member"), None),
        P(("groups", "dp", "member"), None),
        P("member", None),
        P("member", None, None),
        P(("groups", "dp", "member"), None),
    )
    out_specs = (
        P(("groups", "dp", "member"), None),
        P(("groups", "dp", "member"), None),
        P(("groups", "member"), None),
        P(("groups", "member"), "dp", None),
    )
    return jax.shard_map(local, mesh=mesh, in_specs=in_specs, out_specs=out_specs, check_vma=False)
```

```python
import functools

import jax
import jax.numpy as jnp
from jax import lax
from jax.experimental import pallas as pl
from jax.experimental.pallas import tpu as pltpu
from jax.sharding import PartitionSpec as P

POOL = 2
BLOCK = 16
BLK_DEV = 4
CAP = 2


EPS = 1e-06


def gelu_tanh(pre_value):
    return jax.nn.gelu(pre_value, approximate=True)


def slot_table(weights):
    live_mask = (weights > 0).astype(jnp.int32)
    live_rank = jnp.cumsum(live_mask, axis=-1) - 1
    slot_ids = jnp.arange(CAP, dtype=jnp.int32)
    picked = live_mask[..., None, :] * (live_rank[..., None, :] == slot_ids[:, None]).astype(
        jnp.int32
    )
    slot_weight = jnp.sum(picked * weights[..., None, :], axis=-1)
    return (picked, slot_weight)


def head_pass(block_rows, slot_weight, weight, head_count):
    block_rows = block_rows.astype(jnp.float32)
    model_width = block_rows.shape[-1]
    flat_rows = block_rows.reshape(-1, model_width)
    inverse = lax.rsqrt(jnp.mean(flat_rows * flat_rows, axis=-1, keepdims=True) + EPS)
    normed = flat_rows * inverse
    normed_low = normed.astype(jnp.bfloat16)
    pre_act = jnp.dot(normed_low, weight, preferred_element_type=jnp.float32)
    activated, back_act = jax.vjp(gelu_tanh, pre_act)
    pred = (flat_rows + activated).reshape(block_rows.shape)
    error_rows = pred[:, :, :-1] - block_rows[:, :, 1:]
    error_rows = jnp.concatenate([error_rows, jnp.zeros_like(error_rows[:, :, :1])], axis=2)
    row_scale = slot_weight.astype(jnp.float32) / head_count
    d_pred = (error_rows * row_scale[:, :, None, None]).reshape(flat_rows.shape)
    d_pre_low = back_act(d_pred)[0].astype(jnp.bfloat16)
    d_normed = lax.dot_general(
        d_pre_low, weight, (((1,), (1,)), ((), ())), preferred_element_type=jnp.float32
    )
    d_rows = d_pred + inverse * (
        d_normed - normed * jnp.mean(d_normed * normed, axis=-1, keepdims=True)
    )
    return (normed_low, d_pre_low, d_rows.astype(jnp.bfloat16).reshape(block_rows.shape))


def local(context, residual, proj_weight, head_weights, boot):
    members = lax.axis_size("member")
    fits = lax.axis_size("dp") == 4 and lax.axis_size("groups") == 2
    if fits and boot.shape[1] == members == 4 and context.shape[1] % (256 * members) == 0:
        return fused(context, residual, proj_weight, head_weights, boot)
    head_count = boot.shape[1]
    model_width = context.shape[1]
    own_index = lax.axis_index("member")
    whole_proj = lax.all_gather(proj_weight, "member", axis=0, tiled=True)
    hidden = residual.astype(jnp.float32) + jnp.dot(
        context, whole_proj, preferred_element_type=jnp.float32
    )
    latent = jnp.mean(hidden.reshape(BLK_DEV * BLOCK, POOL, model_width), axis=1).astype(
        jnp.bfloat16
    )
    latent = latent.reshape(BLK_DEV, BLOCK, model_width)
    picked_out, weight_out = slot_table(boot.T)
    all_latent, all_boot = (
        lax.all_gather(latent, "member", axis=0, tiled=True),
        lax.all_gather(boot, "member", axis=0, tiled=True),
    )
    own_mask = (jnp.arange(head_count, dtype=jnp.int32) == own_index).astype(jnp.int32)
    column = jnp.sum(all_boot * own_mask[None, :], axis=1).reshape(members, BLK_DEV)
    picked_in, weight_in = slot_table(column)
    all_latent = all_latent.reshape(members, BLK_DEV, BLOCK, model_width)
    received = jnp.einsum(
        "jsk,jkrd->jsrd",
        picked_in.astype(jnp.bfloat16),
        all_latent,
        preferred_element_type=jnp.float32,
    ).astype(jnp.bfloat16)
    weight = head_weights[0]
    normed_low, d_pre_low, d_rows = head_pass(received, weight_in, weight, head_count)
    columns = normed_low
    grad_head = lax.psum_scatter(
        lax.dot_general(
            columns, d_pre_low, (((0,), (0,)), ((), ())), preferred_element_type=jnp.float32
        ).astype(jnp.bfloat16),
        "dp",
        scatter_dimension=0,
        tiled=True,
    ).astype(jnp.float32)
    returned = lax.all_to_all(d_rows, "member", split_axis=0, concat_axis=0, tiled=True)
    grad_latent = jnp.einsum(
        "hsk,hsrd->krd",
        picked_out.astype(jnp.bfloat16),
        returned,
        preferred_element_type=jnp.float32,
    )
    grad_tokens = jnp.broadcast_to(
        grad_latent.reshape(BLK_DEV * BLOCK, 1, model_width) / POOL,
        (BLK_DEV * BLOCK, POOL, model_width),
    )
    grad_low = grad_tokens.reshape(-1, model_width).astype(jnp.bfloat16)
    grad_context = lax.dot_general(
        grad_low, whole_proj, (((1,), (1,)), ((), ())), preferred_element_type=jnp.float32
    )
    columns = context
    grad_proj = lax.psum_scatter(
        lax.dot_general(
            columns, grad_low, (((0,), (0,)), ((), ())), preferred_element_type=jnp.float32
        ).astype(jnp.bfloat16),
        "member",
        scatter_dimension=0,
        tiled=True,
    ).astype(jnp.float32)
    grad_proj = lax.psum(grad_proj.astype(jnp.bfloat16), "dp").astype(jnp.float32)
    return (grad_context.astype(jnp.bfloat16), grad_low, grad_proj, grad_head[None])


MESH = pl.DeviceIdType.MESH
F32 = jnp.float32
BF16 = jnp.bfloat16
LANES = 128
ROW_DEV = BLK_DEV * BLOCK
ROW_SLOT = CAP * BLOCK


def picks(boot_ref, head):
    weights = [boot_ref[k, head] for k in range(BLK_DEV)]
    live = [jnp.where(w > 0, 1, 0) for w in weights]
    factor = [[None] * BLK_DEV for _ in range(CAP)]
    slot = [0] * CAP
    rank = 0
    for k in range(BLK_DEV):
        for s in range(CAP):
            hit = live[k] * jnp.where(rank == s, 1, 0)
            factor[s][k] = hit.astype(F32)
            slot[s] = slot[s] + hit * weights[k]
        rank = rank + live[k]
    return factor, [w.astype(F32) for w in slot]


def step_kernel(
    n,
    context_hbm, residual_hbm, proj_hbm, head_hbm, boot_ref,
    gctx_ref, gres_ref, gproj_ref, ghead_ref,
    context_ref, residual_ref, head_ref,
    whole, pool, poolg, msg, xin, nbuf, ng, dg, dxs, dxin, gg,
    in_sem, z_send, z_recv, pc_send, pc_recv, pf_send, pf_recv, pl_send, pl_recv, co_send, co_recv,
    ms_send, ms_recv, n_send, n_recv, d_send, d_recv, dx_send, dx_recv,
    g_send, g_recv, gx_send, gx_recv, gm_send, gm_recv,
):
    group, dp, me = lax.axis_index("groups"), lax.axis_index("dp"), lax.axis_index("member")
    tokens, width = context_ref.shape
    part = width // n
    cut = part // 8
    core = lax.rem(dp, 2)
    mate = dp + 1 - 2 * core
    across = lax.rem(dp + 2, 4)
    across_mate = lax.rem(mate + 2, 4)
    other = 1 - group
    near = [me + 1 - 2 * lax.rem(me, 2), 2 - me // 2, 3 - 3 * (me // 2)]
    flight = []

    def copy(src, dst, send, recv, g=None, d=None, m=None):
        made = pltpu.make_async_remote_copy(
            src_ref=src, dst_ref=dst, send_sem=send, recv_sem=recv,
            device_id=(group if g is None else g, dp if d is None else d, me if m is None else m),
            device_id_type=MESH,
        )
        made.start()
        flight.append(made)
        return made

    def arrival(dst, send, recv):
        pltpu.make_async_remote_copy(
            src_ref=dst, dst_ref=dst, send_sem=send, recv_sem=recv,
            device_id=(group, mate, me), device_id_type=MESH,
        ).wait_recv()

    def rows_of(owner, g, d, low=0, high=None):
        high = cut if high is None else high
        return pl.ds(pl.multiple_of(owner * part + (g * 4 + d) * cut + low, high - low), high - low)

    def cols(index):
        return pl.ds(pl.multiple_of(index * part, part), part)

    barrier = pltpu.get_barrier_semaphore()
    peers = [(group, dp, m) for m in near]
    peers += [(group, d, me) for d in (mate, across, across_mate)]
    peers += [(other, dp, me)]
    for peer in peers:
        pl.semaphore_signal(barrier, inc=1, device_id=peer, device_id_type=MESH)
    loads = [
        pltpu.make_async_copy(context_hbm, context_ref, in_sem.at[0]),
        pltpu.make_async_copy(residual_hbm, residual_ref, in_sem.at[1]),
        pltpu.make_async_copy(proj_hbm, whole.at[cols(me)], in_sem.at[2]),
        pltpu.make_async_copy(head_hbm.at[0], head_ref, in_sem.at[3]),
    ]
    for load in loads[:3]:
        load.start()
    pl.semaphore_wait(barrier, len(peers))

    own_piece = pl.ds(pl.multiple_of((group * 4 + dp) * cut, cut), cut)
    for i, m in enumerate(near):
        copy(proj_hbm.at[own_piece], whole.at[rows_of(me, group, dp)], z_send.at[i], z_recv.at[me], m=m)
    loads[3].start()
    loads[0].wait()
    loads[1].wait()
    first = lax.broadcasted_iota(jnp.int32, (ROW_DEV, tokens), 0) * 2
    gap = lax.broadcasted_iota(jnp.int32, (ROW_DEV, tokens), 1) - first
    pair = jnp.where((gap >= 0) & (gap < 2), 1.0, 0.0).astype(BF16)
    pool[...] = jnp.dot(pair, context_ref[...], preferred_element_type=F32).astype(BF16)
    poolg[dp, me] = pool[:, cols(me)]

    half = cut // 2
    for i, owner in enumerate(near):
        here = whole.at[rows_of(owner, group, dp)]
        arrival(here, z_send.at[i], z_recv.at[owner])
        copy(here, here, pl_send.at[i, 0], pl_recv.at[owner, 0], d=across)
        copy(here, here, pl_send.at[i, 1], pl_recv.at[owner, 1], g=other)
        copy(here, here, co_send.at[i, 0], co_recv.at[owner, 0], d=mate)
    for i, m in enumerate(near):
        copy(pool.at[:, cols(m)], poolg.at[dp, me], pc_send.at[i], pc_recv.at[me], m=m)
    loads[2].wait()
    total = jnp.dot(pair, residual_ref[...], preferred_element_type=F32)
    total += jnp.dot(pool[:, cols(me)], whole[cols(me), :], preferred_element_type=F32)
    for i, owner in enumerate(near):
        there = whole.at[rows_of(owner, group, across)]
        arrival(there, pl_send.at[i, 0], pl_recv.at[owner, 0])
        low = whole.at[rows_of(owner, group, across, 0, half)]
        copy(low, low, pl_send.at[i, 2], pl_recv.at[owner, 2], g=other)
        copy(there, there, co_send.at[i, 1], co_recv.at[owner, 1], d=mate)
        there = whole.at[rows_of(owner, other, dp)]
        arrival(there, pl_send.at[i, 1], pl_recv.at[owner, 1])
        high = whole.at[rows_of(owner, other, dp, half, cut)]
        copy(high, high, pl_send.at[i, 3], pl_recv.at[owner, 3], d=across)
        copy(there, there, co_send.at[i, 2], co_recv.at[owner, 2], d=mate)
    for i, owner in enumerate(near):
        arrival(whole.at[rows_of(owner, other, across, 0, half)], pl_send.at[i, 2], pl_recv.at[owner, 2])
        arrival(whole.at[rows_of(owner, other, across, half, cut)], pl_send.at[i, 3], pl_recv.at[owner, 3])
        there = whole.at[rows_of(owner, other, across)]
        copy(there, there, co_send.at[i, 3], co_recv.at[owner, 3], d=mate)
    for i, owner in enumerate(near):
        for t, (g, d) in enumerate(((group, mate), (group, across_mate), (other, mate), (other, across_mate))):
            arrival(whole.at[rows_of(owner, g, d)], co_send.at[i, t], co_recv.at[owner, t])
        total += jnp.dot(pool[:, cols(owner)], whole[cols(owner), :], preferred_element_type=F32)
    latent = (total * 0.5).astype(BF16).astype(F32)

    factors = []
    for i, head in list(enumerate(near))[::-1] + [(-1, me)]:
        factor, slot = picks(boot_ref, head)
        factors.append((head, factor))
        for s in range(CAP):
            rows = slice(s * BLOCK, (s + 1) * BLOCK)
            block = factor[s][0] * latent[:BLOCK]
            for k in range(1, BLK_DEV):
                block += factor[s][k] * latent[k * BLOCK : (k + 1) * BLOCK]
            scale = jnp.zeros((BLOCK, LANES), F32) + slot[s]
            if i >= 0:
                msg[i, rows, :width] = block.astype(BF16)
                msg[i, rows, width:] = scale.astype(BF16)
            else:
                xin[me, rows, :width] = block.astype(BF16)
                xin[me, rows, width:] = scale.astype(BF16)
        if i >= 0:
            copy(msg.at[i], xin.at[me], ms_send.at[i], ms_recv.at[me], m=head)

    for i, m in enumerate(near):
        arrival(poolg.at[dp, m], pc_send.at[i], pc_recv.at[m])
    copy(poolg.at[dp], poolg.at[dp], pf_send.at[0], pf_recv.at[0], d=across)
    copy(poolg.at[dp], poolg.at[dp], pf_send.at[1], pf_recv.at[1], d=mate)
    for i, m in enumerate(near):
        arrival(xin.at[m], ms_send.at[i], ms_recv.at[m])

    count = n * ROW_SLOT
    x = xin[:, :, :width].reshape(count, width).astype(F32)
    scale = xin[:, :, width:].reshape(count, LANES).astype(F32)[:, :1] / n
    inverse = lax.rsqrt(jnp.mean(x * x, axis=-1, keepdims=True) + EPS)
    normed = x * inverse
    nbuf[...] = normed.astype(BF16)

    def quarter(d):
        return pl.ds(pl.multiple_of(d * (width // 4), width // 4), width // 4)

    ng[dp] = nbuf[:, quarter(dp)]
    for t, d in enumerate((across, across_mate, mate)):
        copy(nbuf.at[:, quarter(d)], ng.at[dp], n_send.at[t], n_recv.at[t], d=d)
    loads[3].wait()
    pre = jnp.dot(nbuf[...], head_ref[...], preferred_element_type=F32)
    root, cubic = 0.7978845608028654, 0.044715
    bent = jnp.tanh(root * (pre + cubic * pre * pre * pre))
    active = 0.5 * pre * (1.0 + bent)
    slope = 0.5 * (1.0 + bent) + 0.5 * pre * (1.0 - bent * bent) * (root * (1.0 + 3.0 * cubic * pre * pre))
    place = lax.broadcasted_iota(jnp.int32, (count, 1), 0)
    keep = jnp.where((place & (BLOCK - 1)) == BLOCK - 1, 0.0, 1.0)
    after = pltpu.roll(x, count - 1, 0)
    d_pred = (x + active - after) * (scale * keep)
    dg[dp] = (d_pred * slope).astype(BF16)
    copy(dg.at[dp], dg.at[dp], d_send.at[0], d_recv.at[0], d=across)
    copy(dg.at[dp], dg.at[dp], d_send.at[1], d_recv.at[1], d=mate)
    d_normed = lax.dot_general(dg[dp], head_ref[...], (((1,), (1,)), ((), ())), preferred_element_type=F32)
    d_rows = d_pred + inverse * (d_normed - normed * jnp.mean(d_normed * normed, axis=-1, keepdims=True))
    dxs[...] = d_rows.astype(BF16).reshape(n, ROW_SLOT, width)
    dxin[me] = dxs[me]
    for i, m in list(enumerate(near))[::-1]:
        copy(dxs.at[m], dxin.at[me], dx_send.at[i], dx_recv.at[me], m=m)
    arrival(poolg.at[across], pf_send.at[0], pf_recv.at[0])
    copy(poolg.at[across], poolg.at[across], pf_send.at[2], pf_recv.at[2], d=mate)
    arrival(dg.at[across], d_send.at[0], d_recv.at[0])
    copy(dg.at[across], dg.at[across], d_send.at[2], d_recv.at[2], d=mate)
    for i, m in enumerate(near):
        arrival(dxin.at[m], dx_send.at[i], dx_recv.at[m])

    rows = [jnp.zeros((BLOCK, width), F32) for _ in range(BLK_DEV)]
    for head, factor in factors:
        back = dxin[head].astype(F32)
        for k in range(BLK_DEV):
            for s in range(CAP):
                rows[k] += factor[s][k] * back[s * BLOCK : (s + 1) * BLOCK]
    for k in range(BLK_DEV):
        gg[dp, me, k * BLOCK : (k + 1) * BLOCK, :] = (rows[k] * (1.0 / POOL)).astype(BF16)
    own = gg.at[dp, me]
    for i, m in enumerate(near):
        copy(own, own, g_send.at[i], g_recv.at[me], m=m)
    copy(own, own, gx_send.at[n - 1], gx_recv.at[me], d=across)
    copy(own, own, gm_send.at[0, n - 1], gm_recv.at[0, me], d=mate)

    grad = gg[dp, me]
    gres_ref[...] = grad
    gctx = lax.dot_general(grad, whole[...], (((1,), (1,)), ((), ())), preferred_element_type=F32)
    gctx_ref[...] = gctx.astype(BF16)

    def relay(i, m):
        block = gg.at[dp, m]
        arrival(block, g_send.at[i], g_recv.at[m])
        copy(block, block, gx_send.at[i], gx_recv.at[m], d=across)
        copy(block, block, gm_send.at[0, i], gm_recv.at[0, m], d=mate)

    def relay_across(i, m):
        block = gg.at[across, m]
        arrival(block, gx_send.at[i], gx_recv.at[m])
        copy(block, block, gm_send.at[1, i], gm_recv.at[1, m], d=mate)

    relay(0, near[0])
    for t, d in enumerate((across, across_mate, mate)):
        arrival(ng.at[d], n_send.at[t], n_recv.at[t])
    arrival(dg.at[mate], d_send.at[1], d_recv.at[1])
    arrival(dg.at[across_mate], d_send.at[2], d_recv.at[2])
    ghead_ref[0] = lax.dot_general(
        ng[...].reshape(4 * count, width // 4), dg[...].reshape(4 * count, width),
        (((0,), (0,)), ((), ())), preferred_element_type=F32)
    relay(1, near[1])
    relay_across(n - 1, me)
    relay_across(0, near[0])
    relay(2, near[2])
    relay_across(1, near[1])
    relay_across(2, near[2])

    arrival(poolg.at[mate], pf_send.at[1], pf_recv.at[1])
    arrival(poolg.at[across_mate], pf_send.at[2], pf_recv.at[2])
    for i, m in enumerate(list(near) + [me]):
        arrival(gg.at[mate, m], gm_send.at[0, i], gm_recv.at[0, m])
        arrival(gg.at[across_mate, m], gm_send.at[1, i], gm_recv.at[1, m])
    gproj_ref[...] = lax.dot_general(
        poolg[...].reshape(4 * n * ROW_DEV, part), gg[...].reshape(4 * n * ROW_DEV, width),
        (((0,), (0,)), ((), ())), preferred_element_type=F32)
    for made in flight:
        made.wait_send()


def finish_kernel(gctx_in, gres_in, gproj_in, ghead_in, gctx_out, gres_out, gproj_out, ghead_out, wide, sem):
    moves = [
        pltpu.make_async_copy(ghead_in, ghead_out, sem.at[0]),
        pltpu.make_async_copy(gproj_in, gproj_out, sem.at[1]),
    ]
    for move in moves:
        move.start()
    rows = gres_in.shape[0]
    start = lax.broadcasted_iota(jnp.int32, (rows * POOL, rows), 1) * POOL
    gap = lax.broadcasted_iota(jnp.int32, (rows * POOL, rows), 0) - start
    spread = jnp.where((gap >= 0) & (gap < POOL), 1.0, 0.0).astype(BF16)
    for i, (src, dst) in enumerate(((gres_in, gres_out), (gctx_in, gctx_out))):
        wide[i] = jnp.dot(spread, src[...], preferred_element_type=F32).astype(BF16)
        move = pltpu.make_async_copy(wide.at[i], dst, sem.at[2 + i])
        move.start()
        moves.append(move)
    for move in moves:
        move.wait()


def fused(context, residual, proj_weight, head_weights, boot):
    n = lax.axis_size("member")
    tokens, width = context.shape
    count = n * ROW_SLOT
    part = width // n
    hbm = pl.BlockSpec(memory_space=pltpu.HBM)
    vmem = pl.BlockSpec(memory_space=pltpu.VMEM)
    dma = pltpu.SemaphoreType.DMA
    peer, owner = dma((n - 1,)), dma((n,))
    partial = pl.pallas_call(
        functools.partial(step_kernel, n),
        out_shape=(
            pltpu.VMEM((ROW_DEV, width), BF16),
            pltpu.VMEM((ROW_DEV, width), BF16),
            pltpu.VMEM((part, width), F32),
            pltpu.VMEM((1, width // 4, width), F32),
        ),
        in_specs=[hbm] * 4 + [pl.BlockSpec(memory_space=pltpu.SMEM)],
        out_specs=(vmem,) * 4,
        scratch_shapes=[
            pltpu.VMEM((tokens, width), BF16),
            pltpu.VMEM((tokens, width), BF16),
            pltpu.VMEM((width, width), BF16),
            pltpu.VMEM((width, width), BF16),
            pltpu.VMEM((ROW_DEV, width), BF16),
            pltpu.VMEM((4, n, ROW_DEV, part), BF16),
            pltpu.VMEM((n - 1, ROW_SLOT, width + LANES), BF16),
            pltpu.VMEM((n, ROW_SLOT, width + LANES), BF16),
            pltpu.VMEM((count, width), BF16),
            pltpu.VMEM((4, count, width // 4), BF16),
            pltpu.VMEM((4, count, width), BF16),
            pltpu.VMEM((n, ROW_SLOT, width), BF16),
            pltpu.VMEM((n, ROW_SLOT, width), BF16),
            pltpu.VMEM((4, n, ROW_DEV, width), BF16),
            dma((4,)), peer, owner, peer, owner, dma((3,)), dma((3,)),
            dma((n - 1, 4)), dma((n, 4)), dma((n - 1, 4)), dma((n, 4)),
            peer, owner, dma((3,)), dma((3,)), dma((3,)), dma((3,)), peer, owner,
            peer, owner, owner, owner, dma((2, n)), dma((2, n)),
        ],
        compiler_params=pltpu.CompilerParams(
            collective_id=0, has_side_effects=True, vmem_limit_bytes=62900 * 2**10
        ),
        name="step",
    )(context, residual, proj_weight, head_weights, boot)
    return pl.pallas_call(
        finish_kernel,
        out_shape=(
            jax.ShapeDtypeStruct((tokens, width), BF16),
            jax.ShapeDtypeStruct((tokens, width), BF16),
            jax.ShapeDtypeStruct((part, width), F32),
            jax.ShapeDtypeStruct((1, width // 4, width), F32),
        ),
        in_specs=[vmem] * 4,
        out_specs=(hbm,) * 4,
        scratch_shapes=[pltpu.VMEM((2, tokens, width), BF16), dma((4,))],
        compiler_params=pltpu.CompilerParams(vmem_limit_bytes=16 * 2**20),
        name="finish",
    )(*partial)


def solution(mesh):
    in_specs = (
        P(("groups", "dp", "member"), None),
        P(("groups", "dp", "member"), None),
        P("member", None),
        P("member", None, None),
        P(("groups", "dp", "member"), None),
    )
    out_specs = (
        P(("groups", "dp", "member"), None),
        P(("groups", "dp", "member"), None),
        P(("groups", "member"), None),
        P(("groups", "member"), "dp", None),
    )
    return jax.shard_map(local, mesh=mesh, in_specs=in_specs, out_specs=out_specs, check_vma=False)
```

```python
import functools

import jax
import jax.numpy as jnp
from jax import lax
from jax.experimental import pallas as pl
from jax.experimental.pallas import tpu as pltpu
from jax.sharding import PartitionSpec as P

POOL = 2
BLOCK = 16
BLK_DEV = 4
CAP = 2


EPS = 1e-06


def gelu_tanh(pre_value):
    return jax.nn.gelu(pre_value, approximate=True)


def slot_table(weights):
    live_mask = (weights > 0).astype(jnp.int32)
    live_rank = jnp.cumsum(live_mask, axis=-1) - 1
    slot_ids = jnp.arange(CAP, dtype=jnp.int32)
    picked = live_mask[..., None, :] * (live_rank[..., None, :] == slot_ids[:, None]).astype(
        jnp.int32
    )
    slot_weight = jnp.sum(picked * weights[..., None, :], axis=-1)
    return (picked, slot_weight)


def head_pass(block_rows, slot_weight, weight, head_count):
    block_rows = block_rows.astype(jnp.float32)
    model_width = block_rows.shape[-1]
    flat_rows = block_rows.reshape(-1, model_width)
    inverse = lax.rsqrt(jnp.mean(flat_rows * flat_rows, axis=-1, keepdims=True) + EPS)
    normed = flat_rows * inverse
    normed_low = normed.astype(jnp.bfloat16)
    pre_act = jnp.dot(normed_low, weight, preferred_element_type=jnp.float32)
    activated, back_act = jax.vjp(gelu_tanh, pre_act)
    pred = (flat_rows + activated).reshape(block_rows.shape)
    error_rows = pred[:, :, :-1] - block_rows[:, :, 1:]
    error_rows = jnp.concatenate([error_rows, jnp.zeros_like(error_rows[:, :, :1])], axis=2)
    row_scale = slot_weight.astype(jnp.float32) / head_count
    d_pred = (error_rows * row_scale[:, :, None, None]).reshape(flat_rows.shape)
    d_pre_low = back_act(d_pred)[0].astype(jnp.bfloat16)
    d_normed = lax.dot_general(
        d_pre_low, weight, (((1,), (1,)), ((), ())), preferred_element_type=jnp.float32
    )
    d_rows = d_pred + inverse * (
        d_normed - normed * jnp.mean(d_normed * normed, axis=-1, keepdims=True)
    )
    return (normed_low, d_pre_low, d_rows.astype(jnp.bfloat16).reshape(block_rows.shape))


def local(context, residual, proj_weight, head_weights, boot):
    members = lax.axis_size("member")
    fits = lax.axis_size("dp") == 4 and lax.axis_size("groups") == 2
    if fits and boot.shape[1] == members == 4 and context.shape[1] % (256 * members) == 0:
        return fused(context, residual, proj_weight, head_weights, boot)
    head_count = boot.shape[1]
    model_width = context.shape[1]
    own_index = lax.axis_index("member")
    whole_proj = lax.all_gather(proj_weight, "member", axis=0, tiled=True)
    hidden = residual.astype(jnp.float32) + jnp.dot(
        context, whole_proj, preferred_element_type=jnp.float32
    )
    latent = jnp.mean(hidden.reshape(BLK_DEV * BLOCK, POOL, model_width), axis=1).astype(
        jnp.bfloat16
    )
    latent = latent.reshape(BLK_DEV, BLOCK, model_width)
    picked_out, weight_out = slot_table(boot.T)
    all_latent, all_boot = (
        lax.all_gather(latent, "member", axis=0, tiled=True),
        lax.all_gather(boot, "member", axis=0, tiled=True),
    )
    own_mask = (jnp.arange(head_count, dtype=jnp.int32) == own_index).astype(jnp.int32)
    column = jnp.sum(all_boot * own_mask[None, :], axis=1).reshape(members, BLK_DEV)
    picked_in, weight_in = slot_table(column)
    all_latent = all_latent.reshape(members, BLK_DEV, BLOCK, model_width)
    received = jnp.einsum(
        "jsk,jkrd->jsrd",
        picked_in.astype(jnp.bfloat16),
        all_latent,
        preferred_element_type=jnp.float32,
    ).astype(jnp.bfloat16)
    weight = head_weights[0]
    normed_low, d_pre_low, d_rows = head_pass(received, weight_in, weight, head_count)
    columns = normed_low
    grad_head = lax.psum_scatter(
        lax.dot_general(
            columns, d_pre_low, (((0,), (0,)), ((), ())), preferred_element_type=jnp.float32
        ).astype(jnp.bfloat16),
        "dp",
        scatter_dimension=0,
        tiled=True,
    ).astype(jnp.float32)
    returned = lax.all_to_all(d_rows, "member", split_axis=0, concat_axis=0, tiled=True)
    grad_latent = jnp.einsum(
        "hsk,hsrd->krd",
        picked_out.astype(jnp.bfloat16),
        returned,
        preferred_element_type=jnp.float32,
    )
    grad_tokens = jnp.broadcast_to(
        grad_latent.reshape(BLK_DEV * BLOCK, 1, model_width) / POOL,
        (BLK_DEV * BLOCK, POOL, model_width),
    )
    grad_low = grad_tokens.reshape(-1, model_width).astype(jnp.bfloat16)
    grad_context = lax.dot_general(
        grad_low, whole_proj, (((1,), (1,)), ((), ())), preferred_element_type=jnp.float32
    )
    columns = context
    grad_proj = lax.psum_scatter(
        lax.dot_general(
            columns, grad_low, (((0,), (0,)), ((), ())), preferred_element_type=jnp.float32
        ).astype(jnp.bfloat16),
        "member",
        scatter_dimension=0,
        tiled=True,
    ).astype(jnp.float32)
    grad_proj = lax.psum(grad_proj.astype(jnp.bfloat16), "dp").astype(jnp.float32)
    return (grad_context.astype(jnp.bfloat16), grad_low, grad_proj, grad_head[None])


MESH = pl.DeviceIdType.MESH
F32 = jnp.float32
BF16 = jnp.bfloat16
LANES = 128
ROW_DEV = BLK_DEV * BLOCK
ROW_SLOT = CAP * BLOCK


def picks(boot_ref, head):
    weights = [boot_ref[k, head] for k in range(BLK_DEV)]
    live = [jnp.where(w > 0, 1, 0) for w in weights]
    factor = [[None] * BLK_DEV for _ in range(CAP)]
    slot = [0] * CAP
    rank = 0
    for k in range(BLK_DEV):
        for s in range(CAP):
            hit = live[k] * jnp.where(rank == s, 1, 0)
            factor[s][k] = hit.astype(F32)
            slot[s] = slot[s] + hit * weights[k]
        rank = rank + live[k]
    return factor, [w.astype(F32) for w in slot]


def step_kernel(
    n,
    context_hbm, residual_hbm, proj_hbm, head_hbm, boot_ref,
    gctx_ref, gres_ref, gproj_ref, ghead_ref,
    context_ref, residual_ref, head_ref,
    whole, pool, poolg, msg, xin, nbuf, ng, dg, dxs, dxin, gg,
    in_sem, z_send, z_recv, pc_send, pc_recv, pf_send, pf_recv, pl_send, pl_recv, co_send, co_recv,
    ms_send, ms_recv, n_send, n_recv, d_send, d_recv, dx_send, dx_recv,
    g_send, g_recv, gx_send, gx_recv, gm_send, gm_recv,
):
    group, dp, me = lax.axis_index("groups"), lax.axis_index("dp"), lax.axis_index("member")
    tokens, width = context_ref.shape
    part = width // n
    cut = part // 8
    core = lax.rem(dp, 2)
    mate = dp + 1 - 2 * core
    across = lax.rem(dp + 2, 4)
    across_mate = lax.rem(mate + 2, 4)
    other = 1 - group
    near = [me + 1 - 2 * lax.rem(me, 2), 2 - me // 2, 3 - 3 * (me // 2)]
    flight = []

    def copy(src, dst, send, recv, g=None, d=None, m=None):
        made = pltpu.make_async_remote_copy(
            src_ref=src, dst_ref=dst, send_sem=send, recv_sem=recv,
            device_id=(group if g is None else g, dp if d is None else d, me if m is None else m),
            device_id_type=MESH,
        )
        made.start()
        flight.append(made)
        return made

    def arrival(dst, send, recv):
        pltpu.make_async_remote_copy(
            src_ref=dst, dst_ref=dst, send_sem=send, recv_sem=recv,
            device_id=(group, mate, me), device_id_type=MESH,
        ).wait_recv()

    def rows_of(owner, g, d, low=0, high=None):
        high = cut if high is None else high
        return pl.ds(pl.multiple_of(owner * part + (g * 4 + d) * cut + low, high - low), high - low)

    def cols(index):
        return pl.ds(pl.multiple_of(index * part, part), part)

    barrier = pltpu.get_barrier_semaphore()
    peers = [(group, dp, m) for m in near]
    peers += [(group, d, me) for d in (mate, across, across_mate)]
    peers += [(other, dp, me)]
    for peer in peers:
        pl.semaphore_signal(barrier, inc=1, device_id=peer, device_id_type=MESH)
    loads = [
        pltpu.make_async_copy(context_hbm, context_ref, in_sem.at[0]),
        pltpu.make_async_copy(residual_hbm, residual_ref, in_sem.at[1]),
        pltpu.make_async_copy(proj_hbm, whole.at[cols(me)], in_sem.at[2]),
        pltpu.make_async_copy(head_hbm.at[0], head_ref, in_sem.at[3]),
    ]
    for load in loads[:3]:
        load.start()
    pl.semaphore_wait(barrier, len(peers))

    own_piece = pl.ds(pl.multiple_of((group * 4 + dp) * cut, cut), cut)
    for i, m in enumerate(near):
        copy(proj_hbm.at[own_piece], whole.at[rows_of(me, group, dp)], z_send.at[i], z_recv.at[me], m=m)
    loads[3].start()
    loads[0].wait()
    loads[1].wait()
    first = lax.broadcasted_iota(jnp.int32, (ROW_DEV, tokens), 0) * 2
    gap = lax.broadcasted_iota(jnp.int32, (ROW_DEV, tokens), 1) - first
    pair = jnp.where((gap >= 0) & (gap < 2), 1.0, 0.0).astype(BF16)
    pool[...] = jnp.dot(pair, context_ref[...], preferred_element_type=F32).astype(BF16)
    poolg[dp, me] = pool[:, cols(me)]

    half = cut // 2
    for i, owner in enumerate(near):
        here = whole.at[rows_of(owner, group, dp)]
        arrival(here, z_send.at[i], z_recv.at[owner])
        copy(here, here, pl_send.at[i, 0], pl_recv.at[owner, 0], d=across)
        copy(here, here, pl_send.at[i, 1], pl_recv.at[owner, 1], g=other)
        copy(here, here, co_send.at[i, 0], co_recv.at[owner, 0], d=mate)
    for i, m in enumerate(near):
        copy(pool.at[:, cols(m)], poolg.at[dp, me], pc_send.at[i], pc_recv.at[me], m=m)
    loads[2].wait()
    total = jnp.dot(pair, residual_ref[...], preferred_element_type=F32)
    total += jnp.dot(pool[:, cols(me)], whole[cols(me), :], preferred_element_type=F32)
    for i, owner in enumerate(near):
        there = whole.at[rows_of(owner, group, across)]
        arrival(there, pl_send.at[i, 0], pl_recv.at[owner, 0])
        low = whole.at[rows_of(owner, group, across, 0, half)]
        copy(low, low, pl_send.at[i, 2], pl_recv.at[owner, 2], g=other)
        copy(there, there, co_send.at[i, 1], co_recv.at[owner, 1], d=mate)
        there = whole.at[rows_of(owner, other, dp)]
        arrival(there, pl_send.at[i, 1], pl_recv.at[owner, 1])
        high = whole.at[rows_of(owner, other, dp, half, cut)]
        copy(high, high, pl_send.at[i, 3], pl_recv.at[owner, 3], d=across)
        copy(there, there, co_send.at[i, 2], co_recv.at[owner, 2], d=mate)
    for i, owner in enumerate(near):
        arrival(whole.at[rows_of(owner, other, across, 0, half)], pl_send.at[i, 2], pl_recv.at[owner, 2])
        arrival(whole.at[rows_of(owner, other, across, half, cut)], pl_send.at[i, 3], pl_recv.at[owner, 3])
        there = whole.at[rows_of(owner, other, across)]
        copy(there, there, co_send.at[i, 3], co_recv.at[owner, 3], d=mate)
    for i, owner in enumerate(near):
        for t, (g, d) in enumerate(((group, mate), (group, across_mate), (other, mate), (other, across_mate))):
            arrival(whole.at[rows_of(owner, g, d)], co_send.at[i, t], co_recv.at[owner, t])
        total += jnp.dot(pool[:, cols(owner)], whole[cols(owner), :], preferred_element_type=F32)
    latent = (total * 0.5).astype(BF16).astype(F32)

    factors = []
    for i, head in list(enumerate(near))[::-1] + [(-1, me)]:
        factor, slot = picks(boot_ref, head)
        factors.append((head, factor))
        for s in range(CAP):
            rows = slice(s * BLOCK, (s + 1) * BLOCK)
            block = factor[s][0] * latent[:BLOCK]
            for k in range(1, BLK_DEV):
                block += factor[s][k] * latent[k * BLOCK : (k + 1) * BLOCK]
            scale = jnp.zeros((BLOCK, LANES), F32) + slot[s]
            if i >= 0:
                msg[i, rows, :width] = block.astype(BF16)
                msg[i, rows, width:] = scale.astype(BF16)
            else:
                xin[me, rows, :width] = block.astype(BF16)
                xin[me, rows, width:] = scale.astype(BF16)
        if i >= 0:
            copy(msg.at[i], xin.at[me], ms_send.at[i], ms_recv.at[me], m=head)

    for i, m in enumerate(near):
        arrival(poolg.at[dp, m], pc_send.at[i], pc_recv.at[m])
    copy(poolg.at[dp], poolg.at[dp], pf_send.at[0], pf_recv.at[0], d=across)
    copy(poolg.at[dp], poolg.at[dp], pf_send.at[1], pf_recv.at[1], d=mate)
    for i, m in enumerate(near):
        arrival(xin.at[m], ms_send.at[i], ms_recv.at[m])

    count = n * ROW_SLOT
    x = xin[:, :, :width].reshape(count, width).astype(F32)
    scale = xin[:, :, width:].reshape(count, LANES).astype(F32)[:, :1] / n
    inverse = lax.rsqrt(jnp.mean(x * x, axis=-1, keepdims=True) + EPS)
    normed = x * inverse
    nbuf[...] = normed.astype(BF16)

    def quarter(d):
        return pl.ds(pl.multiple_of(d * (width // 4), width // 4), width // 4)

    ng[dp] = nbuf[:, quarter(dp)]
    for t, d in enumerate((across, across_mate, mate)):
        copy(nbuf.at[:, quarter(d)], ng.at[dp], n_send.at[t], n_recv.at[t], d=d)
    loads[3].wait()
    pre = jnp.dot(nbuf[...], head_ref[...], preferred_element_type=F32)
    root, cubic = 0.7978845608028654, 0.044715
    bent = jnp.tanh(root * (pre + cubic * pre * pre * pre))
    active = 0.5 * pre * (1.0 + bent)
    slope = 0.5 * (1.0 + bent) + 0.5 * pre * (1.0 - bent * bent) * (root * (1.0 + 3.0 * cubic * pre * pre))
    place = lax.broadcasted_iota(jnp.int32, (count, 1), 0)
    keep = jnp.where((place & (BLOCK - 1)) == BLOCK - 1, 0.0, 1.0)
    after = pltpu.roll(x, count - 1, 0)
    d_pred = (x + active - after) * (scale * keep)
    dg[dp] = (d_pred * slope).astype(BF16)
    copy(dg.at[dp], dg.at[dp], d_send.at[0], d_recv.at[0], d=across)
    copy(dg.at[dp], dg.at[dp], d_send.at[1], d_recv.at[1], d=mate)
    d_normed = lax.dot_general(dg[dp], head_ref[...], (((1,), (1,)), ((), ())), preferred_element_type=F32)
    d_rows = d_pred + inverse * (d_normed - normed * jnp.mean(d_normed * normed, axis=-1, keepdims=True))
    dxs[...] = d_rows.astype(BF16).reshape(n, ROW_SLOT, width)
    dxin[me] = dxs[me]
    for i, m in list(enumerate(near))[::-1]:
        copy(dxs.at[m], dxin.at[me], dx_send.at[i], dx_recv.at[me], m=m)
    arrival(poolg.at[across], pf_send.at[0], pf_recv.at[0])
    copy(poolg.at[across], poolg.at[across], pf_send.at[2], pf_recv.at[2], d=mate)
    arrival(dg.at[across], d_send.at[0], d_recv.at[0])
    copy(dg.at[across], dg.at[across], d_send.at[2], d_recv.at[2], d=mate)
    for i, m in enumerate(near):
        arrival(dxin.at[m], dx_send.at[i], dx_recv.at[m])

    rows = [jnp.zeros((BLOCK, width), F32) for _ in range(BLK_DEV)]
    for head, factor in factors:
        back = dxin[head].astype(F32)
        for k in range(BLK_DEV):
            for s in range(CAP):
                rows[k] += factor[s][k] * back[s * BLOCK : (s + 1) * BLOCK]
    for k in range(BLK_DEV):
        gg[dp, me, k * BLOCK : (k + 1) * BLOCK, :] = (rows[k] * (1.0 / POOL)).astype(BF16)
    inner = (me == 1) | (me == 2)
    split = ROW_DEV // 2
    passed = []

    def slab(d, m, h):
        return gg.at[d, m, h * split : (h + 1) * split]

    def onward(d, m, h, slot, target):
        block = slab(d, m, h)
        return pltpu.make_async_remote_copy(
            src_ref=block, dst_ref=block, send_sem=g_send.at[slot, h], recv_sem=g_recv.at[m, h],
            device_id=(group, dp, target), device_id_type=MESH)

    def pass_on(*what):
        passed.append(what)
        onward(*what).start()

    def spread_dp(i, m, h):
        block = slab(dp, m, h)
        copy(block, block, gx_send.at[i, h], gx_recv.at[m, h], d=across)
        copy(block, block, gm_send.at[0, i, h], gm_recv.at[0, m, h], d=mate)

    def take(i, m):
        for h in range(2):
            arrival(slab(dp, m, h), g_send.at[i, h], g_recv.at[m, h])

            @pl.when(inner)
            def _():
                pass_on(dp, m, h, 2 + i, near[1] if i == 0 else near[0])

            spread_dp(i, m, h)

    def take_across(i, m):
        for h in range(2):
            block = slab(across, m, h)
            arrival(block, gx_send.at[i, h], gx_recv.at[m, h])
            copy(block, block, gm_send.at[1, i, h], gm_recv.at[1, m, h], d=mate)

    for h in range(2):
        block = slab(dp, me, h)
        copy(block, block, g_send.at[0, h], g_recv.at[me, h], m=near[0])

        @pl.when(inner)
        def _():
            pass_on(dp, me, h, 1, near[1])

        spread_dp(n - 1, me, h)

    grad = gg[dp, me]
    gres_ref[...] = grad
    gctx = lax.dot_general(grad, whole[...], (((1,), (1,)), ((), ())), preferred_element_type=F32)
    gctx_ref[...] = gctx.astype(BF16)
    take(0, near[0])
    for t, d in enumerate((across, across_mate, mate)):
        arrival(ng.at[d], n_send.at[t], n_recv.at[t])
    arrival(dg.at[mate], d_send.at[1], d_recv.at[1])
    arrival(dg.at[across_mate], d_send.at[2], d_recv.at[2])

    def head_part(q):
        lanes = slice(q * (width // 4), (q + 1) * (width // 4))
        ghead_ref[0, :, lanes] = lax.dot_general(
            ng[...].reshape(4 * count, width // 4), dg[:, :, lanes].reshape(4 * count, width // 4),
            (((0,), (0,)), ((), ())), preferred_element_type=F32)

    head_part(0)
    take_across(n - 1, me)
    head_part(1)
    take(1, near[1])
    head_part(2)
    take_across(0, near[0])
    head_part(3)
    take(2, near[2])
    take_across(1, near[1])
    take_across(2, near[2])

    arrival(poolg.at[mate], pf_send.at[1], pf_recv.at[1])
    arrival(poolg.at[across_mate], pf_send.at[2], pf_recv.at[2])
    for i, m in enumerate(list(near) + [me]):
        for h in range(2):
            arrival(slab(mate, m, h), gm_send.at[0, i, h], gm_recv.at[0, m, h])
            arrival(slab(across_mate, m, h), gm_send.at[1, i, h], gm_recv.at[1, m, h])
    gproj_ref[...] = lax.dot_general(
        poolg[...].reshape(4 * n * ROW_DEV, part), gg[...].reshape(4 * n * ROW_DEV, width),
        (((0,), (0,)), ((), ())), preferred_element_type=F32)
    for made in flight:
        made.wait_send()

    @pl.when(inner)
    def _():
        for what in passed:
            onward(*what).wait_send()


def finish_kernel(gctx_in, gres_in, gproj_in, ghead_in, gctx_out, gres_out, gproj_out, ghead_out, wide, sem):
    moves = [
        pltpu.make_async_copy(ghead_in, ghead_out, sem.at[0]),
        pltpu.make_async_copy(gproj_in, gproj_out, sem.at[1]),
    ]
    for move in moves:
        move.start()
    rows = gres_in.shape[0]
    start = lax.broadcasted_iota(jnp.int32, (rows * POOL, rows), 1) * POOL
    gap = lax.broadcasted_iota(jnp.int32, (rows * POOL, rows), 0) - start
    spread = jnp.where((gap >= 0) & (gap < POOL), 1.0, 0.0).astype(BF16)
    for i, (src, dst) in enumerate(((gres_in, gres_out), (gctx_in, gctx_out))):
        wide[i] = jnp.dot(spread, src[...], preferred_element_type=F32).astype(BF16)
        move = pltpu.make_async_copy(wide.at[i], dst, sem.at[2 + i])
        move.start()
        moves.append(move)
    for move in moves:
        move.wait()


def fused(context, residual, proj_weight, head_weights, boot):
    n = lax.axis_size("member")
    tokens, width = context.shape
    count = n * ROW_SLOT
    part = width // n
    hbm = pl.BlockSpec(memory_space=pltpu.HBM)
    vmem = pl.BlockSpec(memory_space=pltpu.VMEM)
    dma = pltpu.SemaphoreType.DMA
    peer, owner = dma((n - 1,)), dma((n,))
    partial = pl.pallas_call(
        functools.partial(step_kernel, n),
        out_shape=(
            pltpu.VMEM((ROW_DEV, width), BF16),
            pltpu.VMEM((ROW_DEV, width), BF16),
            pltpu.VMEM((part, width), F32),
            pltpu.VMEM((1, width // 4, width), F32),
        ),
        in_specs=[hbm] * 4 + [pl.BlockSpec(memory_space=pltpu.SMEM)],
        out_specs=(vmem,) * 4,
        scratch_shapes=[
            pltpu.VMEM((tokens, width), BF16),
            pltpu.VMEM((tokens, width), BF16),
            pltpu.VMEM((width, width), BF16),
            pltpu.VMEM((width, width), BF16),
            pltpu.VMEM((ROW_DEV, width), BF16),
            pltpu.VMEM((4, n, ROW_DEV, part), BF16),
            pltpu.VMEM((n - 1, ROW_SLOT, width + LANES), BF16),
            pltpu.VMEM((n, ROW_SLOT, width + LANES), BF16),
            pltpu.VMEM((count, width), BF16),
            pltpu.VMEM((4, count, width // 4), BF16),
            pltpu.VMEM((4, count, width), BF16),
            pltpu.VMEM((n, ROW_SLOT, width), BF16),
            pltpu.VMEM((n, ROW_SLOT, width), BF16),
            pltpu.VMEM((4, n, ROW_DEV, width), BF16),
            dma((4,)), peer, owner, peer, owner, dma((3,)), dma((3,)),
            dma((n - 1, 4)), dma((n, 4)), dma((n - 1, 4)), dma((n, 4)),
            peer, owner, dma((3,)), dma((3,)), dma((3,)), dma((3,)), peer, owner,
            dma((n + 1, 2)), dma((n, 2)), dma((n, 2)), dma((n, 2)), dma((2, n, 2)), dma((2, n, 2)),
        ],
        compiler_params=pltpu.CompilerParams(
            collective_id=0, has_side_effects=True, vmem_limit_bytes=62900 * 2**10
        ),
        name="step",
    )(context, residual, proj_weight, head_weights, boot)
    return pl.pallas_call(
        finish_kernel,
        out_shape=(
            jax.ShapeDtypeStruct((tokens, width), BF16),
            jax.ShapeDtypeStruct((tokens, width), BF16),
            jax.ShapeDtypeStruct((part, width), F32),
            jax.ShapeDtypeStruct((1, width // 4, width), F32),
        ),
        in_specs=[vmem] * 4,
        out_specs=(hbm,) * 4,
        scratch_shapes=[pltpu.VMEM((2, tokens, width), BF16), dma((4,))],
        compiler_params=pltpu.CompilerParams(vmem_limit_bytes=16 * 2**20),
        name="finish",
    )(*partial)


def solution(mesh):
    in_specs = (
        P(("groups", "dp", "member"), None),
        P(("groups", "dp", "member"), None),
        P("member", None),
        P("member", None, None),
        P(("groups", "dp", "member"), None),
    )
    out_specs = (
        P(("groups", "dp", "member"), None),
        P(("groups", "dp", "member"), None),
        P(("groups", "member"), None),
        P(("groups", "member"), "dp", None),
    )
    return jax.shard_map(local, mesh=mesh, in_specs=in_specs, out_specs=out_specs, check_vma=False)
```
